32 devices in a mesh: cube: 4 (over z), front: 8 (over y, x, core).
Axes of the slice: x: 2, y: 2, z: 4, core: 2. Of those that a mesh axis runs over, the one named last changes fastest.
Arguments:
- right_sides: float32 [3, 4, 512, 128], P(None, 'cube', 'front'), may hold values from -6 to 6
- inverse_leaf: float32 [4, 512, 512], P('cube', 'front'), may hold values from -2 to 2, as said below
- inverse_mid: float32 [4, 512, 1024], P('cube', 'front'), may hold values from -2 to 2, as said below
- inverse_top: float32 [4, 512, 2048], P('cube', 'front'), may hold values from -2 to 2, as said below
- coupling_mid: float32 [4, 512, 1024], P('cube', 'front'), may hold values from -0.25 to 0.25
- coupling_top: float32 [4, 512, 2048], P('cube', 'front'), may hold values from -0.1875 to 0.1875
- pattern_mid: int32 [4, 8, 16], P('cube', 'front'), may hold values 0 or 1
- pattern_top: int32 [4, 8, 32], P('cube', 'front'), may hold values 0 or 1
Outputs:
- solution: float32 [3, 4, 512, 128], P(None, 'cube', 'front')
The draws below stay inside these ranges and needn't reach their ends.
Inputs may be any that keep to these rules, and one draw needn't show every extreme that they name: `inverse_leaf`: each block is the inverse of a lower triangular diagonal block: zero above the diagonal of the separator's row order, diagonal 1 to 2. `inverse_mid`: as inverse_leaf. `inverse_top`: as inverse_leaf.
All inputs are finite; a program needn't handle non-finite values. No bound on the sum of `pattern_mid` or of `pattern_top` on one device may be relied on, other than what follows from the above.
Results may differ from the reference program's by a relative error of at most 0.00013.
Values sent between devices are 32-bit elements; how exact they have to be, the bound alone decides.
No kernel may reach another device: no remote copies, remote signals or barrier semaphores. Data moves between devices by JAX's collectives and lax.ppermute only.
A program may use at most 64 MiB of HBM per device.

```python
import jax
import jax.numpy as jnp
from jax import lax

TILE = 64
NRHS = 128
LEVELS = 3
SEP = 512
N_CUBE = 4


def lower_block(key, members):
    width = members * SEP
    key_noise, key_diag = jax.random.split(key, 2)
    node_row = ((jnp.arange(N_CUBE) % members)[:, None] * SEP + jnp.arange(SEP)[None, :])[:, :, None]
    column = jnp.arange(width)[None, None, :]
    noise = jnp.clip(jax.random.normal(key_noise, (N_CUBE, SEP, width), jnp.float32), -6.0, 6.0)
    off_diag = noise * (0.5 / width ** 0.5)
    diagonal = 1.0 + jax.random.uniform(key_diag, (N_CUBE, SEP, 1), jnp.float32)
    lower = jnp.where(column < node_row, off_diag, 0.0)
    return lower + jnp.where(column == node_row, diagonal, 0.0)


def draw_inverse_leaf(key, part):
    return lower_block(jax.random.fold_in(key, 11), 1)


def draw_inverse_mid(key, part):
    return lower_block(jax.random.fold_in(key, 12), 2)


def draw_inverse_top(key, part):
    return lower_block(jax.random.fold_in(key, 13), 4)


def plant(drawn, rng, smallest, top_value):
    longest = drawn.shape.index(max(drawn.shape))
    spots = []
    for shift in (0, 1):
        where = [jax.random.randint(jax.random.fold_in(rng, axis), (), 0, length) for axis, length in enumerate(drawn.shape)]
        where[longest] = (where[longest] + shift) % drawn.shape[longest]
        spots.append(tuple(where))
    return drawn.at[spots[0]].set(smallest).at[spots[1]].set(top_value)


def raised(entries, own_key, source, target, blocks, factor):
    def block_of(dim):
        return (jnp.arange(entries.shape[dim]) // (entries.shape[dim] // blocks)).reshape((-1,) + (1,) * (entries.ndim - 1 - dim))

    one_side = jax.random.permutation(own_key, blocks)[block_of(target)]
    second = (block_of(target) + blocks // 2) % blocks
    return jnp.where((block_of(source) == one_side) | (block_of(source) == second), factor * entries, entries)


def block_scale(own_key, dims, cuts, low, largest):
    loudness = 1.0
    for position, parts in cuts:
        heights = jax.random.uniform(jax.random.fold_in(jax.random.fold_in(own_key, 6), position), (parts,), jnp.float32, low / len(cuts), largest / len(cuts))
        loudness = loudness * jnp.repeat(jnp.exp(heights), dims[position] // parts).reshape((-1,) + (1,) * (len(dims) - 1 - position))
    return loudness


def bell_draw(key, dims, scale, most, cuts=(), kind=jnp.bfloat16):
    level = block_scale(key, dims, cuts, -0.22, 0.18) if cuts else 1.0
    drawn = jax.random.normal(key, dims, jnp.float32) * scale * level
    return jnp.minimum(jnp.maximum(drawn, -most), most).astype(kind)


def noise_with(key, shape, scale, limit, pieces, heavy, dtype=jnp.bfloat16):
    result = scale * jax.random.normal(key, shape, jnp.float32)
    if pieces:
        result = result * block_scale(key, shape, pieces, -0.22, 0.18)
    return jnp.clip(raised(result, jax.random.fold_in(key, 3), *heavy), -limit, limit).astype(dtype)


def setup_inputs(seed: int = 0) -> dict:
    streams_of = jax.random.split(jax.random.key(seed), 9)
    return {
        "right_sides": bell_draw(streams_of[0], (LEVELS, N_CUBE, SEP, NRHS), 1.0, 6.0, ((1, 4), (2, 8)), jnp.float32),
        "inverse_leaf": draw_inverse_leaf(jax.random.fold_in(streams_of[8], 71), 0),
        "inverse_mid": draw_inverse_mid(jax.random.fold_in(streams_of[8], 71), 0),
        "inverse_top": draw_inverse_top(jax.random.fold_in(streams_of[8], 71), 0),
        "coupling_mid": noise_with(streams_of[4], (N_CUBE, SEP, 2 * SEP), (2 * SEP) ** -0.5, 0.25, ((0, 4), (1, 8)), (1, 2, 8, 2.0), jnp.float32),
        "coupling_top": noise_with(streams_of[5], (N_CUBE, SEP, 4 * SEP), (4 * SEP) ** -0.5, 0.1875, ((0, 4), (1, 8)), (1, 2, 8, 2.0), jnp.float32),
        "pattern_mid": plant((jax.random.randint(streams_of[6], (N_CUBE, SEP // TILE, 2 * SEP // TILE), 0, 4) < 3).astype(jnp.int32), jax.random.fold_in(streams_of[6], 1), 0, 1),
        "pattern_top": plant((jax.random.randint(streams_of[7], (N_CUBE, SEP // TILE, 4 * SEP // TILE), 0, 4) < 3).astype(jnp.int32), jax.random.fold_in(streams_of[7], 1), 0, 1),
    }


def masked(coupling, pattern):
    keep_rows = jnp.repeat(pattern, TILE, axis=1)
    keep_all = jnp.repeat(keep_rows, TILE, axis=2)
    return coupling * keep_all.astype(jnp.float32)


def grouped(array, members):
    return array.reshape(N_CUBE // members, members * array.shape[1], array.shape[2])


def flatten(array):
    return array.reshape(N_CUBE, SEP, array.shape[2])


def product(matrix, vector):
    return jnp.einsum("nij,njk->nik", matrix, vector, precision=lax.Precision.HIGHEST)


def transposed(matrix, vector):
    return jnp.einsum("nji,njk->nik", matrix, vector, precision=lax.Precision.HIGHEST)


def reference(right_sides, inverse_leaf, inverse_mid, inverse_top, coupling_mid, coupling_top, pattern_mid, pattern_top):
    block_mid = grouped(masked(coupling_mid, pattern_mid), 2)
    block_top = grouped(masked(coupling_top, pattern_top), 4)
    inv_leaf = grouped(inverse_leaf, 1)
    inv_mid = grouped(inverse_mid, 2)
    inv_top = grouped(inverse_top, 4)
    solved_leaf = product(inv_leaf, grouped(right_sides[0], 1))
    update_mid = product(block_mid, grouped(flatten(solved_leaf), 2))
    solved_mid = product(inv_mid, grouped(right_sides[1], 2) - update_mid)
    update_top = product(block_top, grouped(flatten(solved_mid), 4))
    solved_top = product(inv_top, grouped(right_sides[2], 4) - update_top)
    back_top = transposed(inv_top, solved_top)
    carry_mid = grouped(flatten(transposed(block_top, back_top)), 2)
    back_mid = transposed(inv_mid, solved_mid - carry_mid)
    carry_leaf = grouped(flatten(transposed(block_mid, back_mid)), 1)
    back_leaf = transposed(inv_leaf, solved_leaf - carry_leaf)
    return jnp.stack([flatten(back_leaf), flatten(back_mid), flatten(back_top)])
```

```python
import jax
import jax.numpy as jnp
from jax import lax
from jax.sharding import PartitionSpec as P

TILE = 64


def exchange(value, axis, mask):
    pairs = [(source, source ^ mask) for source in range(lax.axis_size(axis))]
    return lax.ppermute(value, axis, pairs)


def masked(coupling, pattern):
    keep = jnp.repeat(pattern[0, 0], TILE)
    return coupling[0] * keep.astype(jnp.float32)


def absolute(pieces, index):
    stacked = jnp.stack(pieces)
    count = len(pieces)
    bit = 1
    while bit < count:
        swapped = jnp.stack([stacked[m ^ bit] for m in range(count)])
        stacked = jnp.where(index // bit % 2 == 0, stacked, swapped)
        bit *= 2
    return stacked


def swap_slices(matrix, parts, index, axis, unit):
    pieces = []
    for m in range(parts):
        piece = lax.dynamic_index_in_dim(matrix, index ^ m, 1, keepdims=False)
        pieces.append(piece if m == 0 else exchange(piece, axis, m * unit))
    return absolute(pieces, index)


def gather_team(block, team, index):
    pieces = [block]
    bit = team // 2
    order = [0]
    while bit:
        pieces += [exchange(piece, "front", bit) for piece in pieces]
        order += [m | bit for m in order]
        bit //= 2
    return absolute([pieces[order.index(m)] for m in range(team)], index)


def summed(value, axis, count, unit):
    bit = 1
    while bit < count:
        value = value + exchange(value, axis, bit * unit)
        bit *= 2
    return value


def times_rows(vector, matrix):
    return lax.dot_general(
        vector, matrix, (((1,), (1,)), ((), ())), precision=lax.Precision.HIGH,
        preferred_element_type=jnp.float32,
    )


def times(vector, matrix):
    return lax.dot_general(
        vector, matrix, (((1,), (0,)), ((), ())), precision=lax.Precision.HIGH,
        preferred_element_type=jnp.float32,
    )


def local(
    right_sides,
    inverse_leaf,
    inverse_mid,
    inverse_top,
    coupling_mid,
    coupling_top,
    pattern_mid,
    pattern_top,
):
    front = lax.axis_size("front")
    cube_pos = lax.axis_index("cube")
    front_pos = lax.axis_index("front")
    team = min(4, front)
    parts = front // team
    g, q = front_pos % team, front_pos // team
    levels, _, rows, columns = right_sides.shape
    width = columns // team
    half = team * rows
    groups = [[base * team + m for m in range(team)] for base in range(parts)]

    def inverse_block(inverse, count):
        shaped = inverse[0].reshape(rows, count, parts, half)
        shaped = jnp.moveaxis(shaped, 2, 1)
        swapped = swap_slices(shaped, parts, q, "front", team)
        whole = gather_team(swapped, team, g)
        return jnp.moveaxis(whole, 0, 1).reshape(front * rows, count * half)

    def coupling_block(coupling, pattern, count):
        shaped = masked(coupling, pattern).reshape(rows, count, front * rows)
        swapped = swap_slices(shaped, count, cube_pos % count, "cube", 1)
        whole = gather_team(swapped, team, g)
        return jnp.moveaxis(whole, 0, 1).reshape(count * half, front * rows)

    def own_rows(side, count):
        here = lax.broadcasted_iota(jnp.int32, (1, count, 1), 1) == cube_pos % count
        return jnp.where(here, side[:, None], 0.0).reshape(width, count * half)

    def pick(value, count):
        shaped = value.reshape(width, count, half)
        return lax.dynamic_index_in_dim(shaped, cube_pos % count, 1, keepdims=False)

    sides = jnp.swapaxes(right_sides[:, 0], 1, 2).reshape(levels, team, width, rows)
    sides = lax.all_to_all(sides, "front", 1, 1, axis_index_groups=groups)
    sides = jnp.moveaxis(sides, 1, 2).reshape(levels, width, half)

    leaf = inverse_block(inverse_leaf, 1)
    couple_mid = coupling_block(coupling_mid, pattern_mid, 2)
    mid = inverse_block(inverse_mid, 2)
    couple_top = coupling_block(coupling_top, pattern_top, 4)
    top = inverse_block(inverse_top, 4)

    y0 = summed(times_rows(sides[0], leaf), "front", parts, team)
    w1 = summed(own_rows(sides[1], 2) - times_rows(y0, couple_mid), "cube", 2, 1)
    y1 = summed(times_rows(w1, mid), "front", parts, team)
    w2 = summed(own_rows(sides[2], 4) - times_rows(y1, couple_top), "cube", 4, 1)
    y2 = summed(times_rows(w2, top), "front", parts, team)
    x2 = summed(times(y2, top), "cube", 4, 1)
    c1 = summed(times(x2, couple_top), "front", parts, team)
    x1 = summed(times(y1 - c1, mid), "cube", 2, 1)
    c0 = summed(times(x1, couple_mid), "front", parts, team)
    x0 = times(y0 - c0, leaf)

    found = jnp.stack([x0, pick(x1, 2), pick(x2, 4)])
    found = jnp.moveaxis(found.reshape(levels, width, team, rows), 2, 1)
    found = lax.all_to_all(found, "front", 1, 1, axis_index_groups=groups)
    found = jnp.swapaxes(found.reshape(levels, columns, rows), 1, 2)
    return found[:, None]


def solution(mesh):
    return jax.shard_map(
        local,
        mesh=mesh,
        in_specs=(
            P(None, "cube", "front", None),
            P("cube", "front", None),
            P("cube", "front", None),
            P("cube", "front", None),
            P("cube", "front", None),
            P("cube", "front", None),
            P("cube", "front", None),
            P("cube", "front", None),
        ),
        out_specs=P(None, "cube", "front", None),
        check_vma=False,
    )
```

```python
import functools

import jax
import jax.numpy as jnp
from jax import lax
from jax.experimental import pallas as pl
from jax.experimental.pallas import tpu as pltpu
from jax.sharding import PartitionSpec as P

TILE = 64
TEAM = 4
F32, BF16 = jnp.float32, jnp.bfloat16


def exchange(value, axis, mask):
    pairs = [(source, source ^ mask) for source in range(lax.axis_size(axis))]
    return lax.ppermute(value, axis, pairs)


def call(kernel, outs, *operands, scratch=()):
    smem = pl.BlockSpec(memory_space=pltpu.SMEM)
    vmem = pl.BlockSpec(memory_space=pltpu.VMEM)
    specs = [smem if value.dtype == jnp.int32 else vmem for value in operands]
    return pl.pallas_call(
        kernel,
        out_shape=[jax.ShapeDtypeStruct(shape, dtype) for shape, dtype in outs],
        in_specs=specs,
        out_specs=[vmem] * len(outs),
        scratch_shapes=list(scratch),
    )(*operands)


def split(value):
    high = value.astype(BF16)
    return high, (value - high.astype(F32)).astype(BF16)


def product(value, high, low, contract):
    dims = (((1,), (contract,)), ((), ()))
    dot = functools.partial(lax.dot_general, dimension_numbers=dims, preferred_element_type=F32)
    first, second = split(value)
    return dot(first, high) + (dot(second, high) + dot(first, low))


def team_order(pieces, g):
    join = lambda a, b: jnp.concatenate([a, b], axis=-1)
    inner = [
        jnp.where(g % 2 == 0, join(pieces[m], pieces[m + 1]), join(pieces[m + 1], pieces[m]))
        for m in (0, 2)
    ]
    return jnp.where(g // 2 == 0, join(*inner), join(inner[1], inner[0]))


def team_pieces(value, g):
    half = value.shape[-1] // 2
    sides = value[..., :half], value[..., half:]
    pieces = []
    for first, second in (sides, sides[::-1]):
        same = jnp.where(g // 2 == 0, first, second)
        parts = same[..., : half // 2], same[..., half // 2 :]
        for a, b in (parts, parts[::-1]):
            pieces.append(jnp.where(g % 2 == 0, a, b))
    return pieces


def slice_columns(matrix, outs, index, blocks):
    parts, width = len(outs), outs[0].shape[1] // blocks
    for m, out in enumerate(outs):
        for block in range(blocks):
            start = pl.multiple_of((block * parts + (index ^ m)) * width, 128)
            out[:, block * width : (block + 1) * width] = matrix[0, :, pl.ds(start, width)]


def slice_masked(matrix, pattern, outs, index):
    _, width = outs[0].shape
    lane = lax.broadcasted_iota(jnp.int32, (1, 128), 1)
    for m, out in enumerate(outs):
        start = (index ^ m) * width
        for block in range(width // 128):
            at = pl.multiple_of(start + block * 128, 128)
            keep = jnp.zeros((1, 128), F32)
            for tile in range(128 // TILE):
                bit = pattern[0, 0, (start + block * 128) // TILE + tile].astype(F32)
                keep = jnp.where(lane // TILE == tile, bit, keep)
            out[:, block * 128 : (block + 1) * 128] = matrix[0, :, pl.ds(at, 128)] * keep


def prepare_leaf(place, matrix, sides, *rest):
    parts = len(rest) - 1 - TEAM
    outs, pieces, turned = rest[:parts], rest[parts:-1], rest[-1]
    g, q = place[0], place[1]
    slice_columns(matrix, outs, q, 1)
    for level in range(sides.shape[0]):
        turned[level] = sides[level, 0].T
    width = turned.shape[1] // TEAM
    for m, piece in enumerate(pieces):
        start = pl.multiple_of((g ^ m) * width, 8)
        piece[...] = turned[:, pl.ds(start, width), :]


def prepare_level(slot, count, place, coupling, pattern, inverse, *outs):
    slice_masked(coupling, pattern, outs[:count], place[slot])
    slice_columns(inverse, outs[count:], place[1], count)


def assemble(slot, rows, place, own, across, beside, both, high, low):
    g, index = place[0], place[slot]
    for m_team, piece in ((0, own), (2, across), (1, beside), (3, both)):
        for m in range(piece.shape[0] // rows):
            at = pl.multiple_of(((index ^ m) * TEAM + (g ^ m_team)) * rows, rows)
            first, second = split(piece[m * rows : (m + 1) * rows])
            high[pl.ds(at, rows), :] = first
            low[pl.ds(at, rows), :] = second


def start_kernel(place, p0, p1, p2, p3, high, low, out, *sides):
    whole = team_order([p[...] for p in (p0, p1, p2, p3)], place[0])
    out[...] = product(whole[0], high[...], low[...], 1)
    for level, side in enumerate(sides):
        side[...] = whole[level + 1]


def couple_kernel(slot, place, own, got, side, high, low, total, out):
    total[...] = own[...] + got[...]
    out[...] = -product(total[...], high[...], low[...], 1)
    half = side.shape[1]
    at = pl.ds(pl.multiple_of(place[slot] * half, 128), half)
    out[:, at] = out[:, at] + side[...]


def forward_kernel(own, got, high, low, out):
    out[...] = product(own[...] + got[...], high[...], low[...], 1)


def backward_kernel(own, got, high, low, out):
    out[...] = product(own[...] + got[...], high[...], low[...], 0)


def carry_top_kernel(place, own, got, high, low, out, mine, total):
    total[...] = own[...] + got[...]
    out[...] = product(total[...], high[...], low[...], 0)
    half = mine.shape[1]
    mine[...] = total[:, pl.ds(pl.multiple_of(place[3] * half, 128), half)]


def subtract_kernel(solved, own, got, high, low, out):
    out[...] = product(solved[...] - (own[...] + got[...]), high[...], low[...], 0)


def carry_mid_kernel(place, own, got, top, high, low, out, *rest):
    pieces, total = rest[:-1], rest[-1]
    total[...] = own[...] + got[...]
    out[...] = product(total[...], high[...], low[...], 0)
    half = top.shape[1]
    mid = total[:, pl.ds(pl.multiple_of(place[2] * half, 128), half)]
    for level, value in enumerate((mid, top[...])):
        for piece, part in zip(pieces, team_pieces(value, place[0])):
            piece[level] = part


def finish_kernel(place, solved, own, got, high, low, *pieces):
    leaf = product(solved[...] - (own[...] + got[...]), high[...], low[...], 0)
    for piece, part in zip(pieces, team_pieces(leaf, place[0])):
        piece[...] = part


def output_kernel(place, *rest):
    leaf, upper, out, turned = rest[:TEAM], rest[TEAM : 2 * TEAM], rest[-2], rest[-1]
    width = leaf[0].shape[0]
    for m in range(TEAM):
        at = pl.ds(pl.multiple_of((place[0] ^ m) * width, 8), width)
        turned[0, at, :] = leaf[m][...]
        turned[1:, at, :] = upper[m][...]
    for level in range(out.shape[0]):
        out[level, 0] = turned[level].T


def local(
    right_sides,
    inverse_leaf,
    inverse_mid,
    inverse_top,
    coupling_mid,
    coupling_top,
    pattern_mid,
    pattern_top,
):
    front = lax.axis_size("front")
    cube_pos, front_pos = lax.axis_index("cube"), lax.axis_index("front")
    parts = front // TEAM
    levels, _, rows, columns = right_sides.shape
    width, half, full = columns // TEAM, TEAM * rows, front * rows
    group_mid, group_top = inverse_mid.shape[2] // full, inverse_top.shape[2] // full
    place = jnp.stack([front_pos % TEAM, front_pos // TEAM, cube_pos % group_mid, cube_pos % group_top])

    def to_parts(pieces, axis, unit):
        return [
            piece if m == 0 else exchange(piece, axis, m * unit)
            for m, piece in enumerate(pieces)
        ]

    def whole_block(own, across, slot):
        if across is None:
            across = exchange(own, "front", 2)
        beside = exchange(own, "front", 1)
        both = exchange(across, "front", 1)
        shape = (TEAM * own.shape[0], own.shape[1])
        return call(
            functools.partial(assemble, slot, rows), [(shape, BF16)] * 2,
            place, own, across, beside, both,
        )

    def partial_sum(value, axis, count, unit):
        got, bit = jnp.zeros_like(value), 1
        while bit < count:
            if bit > 1:
                value = value + got
            got = exchange(value, axis, bit * unit)
            bit *= 2
        return value, got

    out = call(
        prepare_leaf,
        [((rows, half), F32)] * parts + [((levels, width, rows), F32)] * TEAM,
        place, inverse_leaf, right_sides,
        scratch=[pltpu.VMEM((levels, columns, rows), F32)],
    )
    leaf_pieces, side_pieces = out[:parts], out[parts:]
    leaf_own = jnp.concatenate(to_parts(leaf_pieces, "front", TEAM))
    leaf_across = jnp.concatenate([
        exchange(piece, "front", m * TEAM + 2) for m, piece in enumerate(leaf_pieces)
    ])
    sides = to_parts(side_pieces, "front", 1)
    leaf = whole_block(leaf_own, leaf_across, 1)

    blocks = []
    for slot, count, coupling, pattern, inverse in (
        (2, group_mid, coupling_mid, pattern_mid, inverse_mid),
        (3, group_top, coupling_top, pattern_top, inverse_top),
    ):
        out = call(
            functools.partial(prepare_level, slot, count),
            [((rows, full), F32)] * count + [((rows, count * half), F32)] * parts,
            place, coupling, pattern, inverse,
        )
        couple_own = jnp.concatenate(to_parts(out[:count], "cube", 1))
        own = jnp.concatenate(to_parts(out[count:], "front", TEAM))
        blocks.append(whole_block(couple_own, None, slot))
        blocks.append(whole_block(own, None, 1))
    couple_mid, mid, couple_top, top = blocks

    vector = lambda n: ((width, n), F32)
    y0, side_mid, side_top = call(
        start_kernel, [vector(full), vector(half), vector(half)], place, *sides, *leaf,
    )
    y0 = partial_sum(y0, "front", parts, TEAM)
    y0, w1 = call(
        functools.partial(couple_kernel, 2), [vector(full), vector(group_mid * half)],
        place, *y0, side_mid, *couple_mid,
    )
    w1 = partial_sum(w1, "cube", group_mid, 1)
    y1, = call(forward_kernel, [vector(full)], *w1, *mid)
    y1 = partial_sum(y1, "front", parts, TEAM)
    y1, w2 = call(
        functools.partial(couple_kernel, 3), [vector(full), vector(group_top * half)],
        place, *y1, side_top, *couple_top,
    )
    w2 = partial_sum(w2, "cube", group_top, 1)
    y2, = call(forward_kernel, [vector(full)], *w2, *top)
    y2 = partial_sum(y2, "front", parts, TEAM)
    x2, = call(backward_kernel, [vector(group_top * half)], *y2, *top)
    x2 = partial_sum(x2, "cube", group_top, 1)
    c1, mine = call(
        carry_top_kernel, [vector(full), vector(half)], place, *x2, *couple_top,
        scratch=[pltpu.VMEM((width, group_top * half), F32)],
    )
    c1 = partial_sum(c1, "front", parts, TEAM)
    x1, = call(subtract_kernel, [vector(group_mid * half)], y1, *c1, *mid)
    x1 = partial_sum(x1, "cube", group_mid, 1)
    c0, *upper = call(
        carry_mid_kernel, [vector(full)] + [((2, width, rows), F32)] * TEAM,
        place, *x1, mine, *couple_mid,
        scratch=[pltpu.VMEM((width, group_mid * half), F32)],
    )
    c0 = partial_sum(c0, "front", parts, TEAM)
    upper = to_parts(upper, "front", 1)
    found = call(finish_kernel, [vector(rows)] * TEAM, place, y0, *c0, *leaf)
    found = to_parts(found, "front", 1)
    result, = call(
        output_kernel, [((levels, 1, rows, columns), F32)], place, *found, *upper,
        scratch=[pltpu.VMEM((levels, columns, rows), F32)],
    )
    return result


def solution(mesh):
    return jax.shard_map(
        local,
        mesh=mesh,
        in_specs=(
            P(None, "cube", "front", None),
            P("cube", "front", None),
            P("cube", "front", None),
            P("cube", "front", None),
            P("cube", "front", None),
            P("cube", "front", None),
            P("cube", "front", None),
            P("cube", "front", None),
        ),
        out_specs=P(None, "cube", "front", None),
        check_vma=False,
    )
```

```python
import jax
import jax.numpy as jnp
from jax import lax
from jax.sharding import PartitionSpec as P

TILE = 64
TEAM = 4


def exchange(value, axis, mask):
    pairs = [(source, source ^ mask) for source in range(lax.axis_size(axis))]
    return lax.ppermute(value, axis, pairs)


def absolute(pieces, index, axis=0):
    count, bit = len(pieces), 1
    while bit < count:
        pieces = [
            jnp.where(index // bit % 2 == 0, pieces[m], pieces[m ^ bit]) for m in range(count)
        ]
        bit *= 2
    return jnp.stack(pieces, axis)


def team_order(pieces, g):
    join = lambda a, b: jnp.concatenate([a, b], axis=-1)
    inner = [
        jnp.where(g % 2 == 0, join(pieces[m], pieces[m + 1]), join(pieces[m + 1], pieces[m]))
        for m in (0, 2)
    ]
    return jnp.where(g // 2 == 0, join(*inner), join(inner[1], inner[0]))


def team_pieces(value, g):
    half = value.shape[-1] // 2
    sides = value[..., :half], value[..., half:]
    pieces = []
    for first, second in (sides, sides[::-1]):
        same = jnp.where(g // 2 == 0, first, second)
        parts = same[..., : half // 2], same[..., half // 2 :]
        for a, b in (parts, parts[::-1]):
            pieces.append(jnp.where(g % 2 == 0, a, b))
    return pieces


def to_parts(pieces, axis, unit):
    return [piece if m == 0 else exchange(piece, axis, m * unit) for m, piece in enumerate(pieces)]


def summed(value, axis, count, unit):
    bit = 1
    while bit < count:
        value = value + exchange(value, axis, bit * unit)
        bit *= 2
    return value


def times(vector, matrix, contract):
    return lax.dot_general(
        vector, matrix, (((1,), (contract,)), ((), ())), precision=lax.Precision.HIGHEST,
        preferred_element_type=jnp.float32,
    )


def local(
    right_sides,
    inverse_leaf,
    inverse_mid,
    inverse_top,
    coupling_mid,
    coupling_top,
    pattern_mid,
    pattern_top,
):
    front = lax.axis_size("front")
    cube_pos, front_pos = lax.axis_index("cube"), lax.axis_index("front")
    parts = front // TEAM
    g, q = front_pos % TEAM, front_pos // TEAM
    _, _, rows, columns = right_sides.shape
    width, half, full = columns // TEAM, TEAM * rows, front * rows
    group_mid, group_top = inverse_mid.shape[2] // full, inverse_top.shape[2] // full

    def inverse_pieces(inverse, count):
        return [
            jnp.concatenate([
                lax.dynamic_slice_in_dim(inverse[0], (block * parts + (q ^ m)) * half, half, 1)
                for block in range(count)
            ], axis=1)
            for m in range(parts)
        ]

    def coupling_pieces(coupling, pattern, count):
        keep = jnp.repeat(pattern[0].astype(jnp.float32), TILE, axis=1)
        starts = [(cube_pos % count ^ m) * full for m in range(count)]
        return [
            lax.dynamic_slice_in_dim(coupling[0], start, full, 1)
            * lax.dynamic_slice_in_dim(keep, start, full, 1)
            for start in starts
        ]

    def whole_block(own, across):
        if across is None:
            across = exchange(own, "front", 2)
        beside = exchange(own, "front", 1)
        both = exchange(across, "front", 1)
        whole = absolute([own, beside, across, both], g, axis=1)
        return whole.reshape(TEAM * own.shape[0] * rows, own.shape[2])

    def inverse_block(inverse, count):
        pieces = inverse_pieces(inverse, count)
        own = absolute(to_parts(pieces, "front", TEAM), q)
        return whole_block(own, None)

    def coupling_block(coupling, pattern, count):
        pieces = coupling_pieces(coupling, pattern, count)
        own = absolute(to_parts(pieces, "cube", 1), cube_pos % count)
        return whole_block(own, None)

    def own_rows(side, count):
        here = lax.broadcasted_iota(jnp.int32, (1, count, 1), 1) == cube_pos % count
        return jnp.where(here, side[:, None], 0.0).reshape(width, count * half)

    def pick(value, count):
        return lax.dynamic_slice_in_dim(value, cube_pos % count * half, half, 1)

    def rows_back(value):
        pieces = to_parts(team_pieces(value, g), "front", 1)
        turned = absolute(pieces, g, axis=1).reshape(value.shape[0], columns, rows)
        return jnp.swapaxes(turned, 1, 2)

    pieces = inverse_pieces(inverse_leaf, 1)
    own = absolute(to_parts(pieces, "front", TEAM), q)
    across = absolute([exchange(piece, "front", m * TEAM + 2) for m, piece in enumerate(pieces)], q)
    turned = jnp.swapaxes(right_sides[:, 0], 1, 2)
    sides = team_order(to_parts([
        lax.dynamic_slice_in_dim(turned, (g ^ m) * width, width, 1) for m in range(TEAM)
    ], "front", 1), g)

    leaf = whole_block(own, across)
    couple_mid = coupling_block(coupling_mid, pattern_mid, group_mid)
    mid = inverse_block(inverse_mid, group_mid)
    couple_top = coupling_block(coupling_top, pattern_top, group_top)
    top = inverse_block(inverse_top, group_top)

    y0 = summed(times(sides[0], leaf, 1), "front", parts, TEAM)
    w1 = own_rows(sides[1], group_mid) - times(y0, couple_mid, 1)
    w1 = summed(w1, "cube", group_mid, 1)
    y1 = summed(times(w1, mid, 1), "front", parts, TEAM)
    w2 = own_rows(sides[2], group_top) - times(y1, couple_top, 1)
    w2 = summed(w2, "cube", group_top, 1)
    y2 = summed(times(w2, top, 1), "front", parts, TEAM)
    x2 = summed(times(y2, top, 0), "cube", group_top, 1)
    c1 = summed(times(x2, couple_top, 0), "front", parts, TEAM)
    x1 = summed(times(y1 - c1, mid, 0), "cube", group_mid, 1)
    c0 = summed(times(x1, couple_mid, 0), "front", parts, TEAM)
    upper = rows_back(jnp.stack([pick(x1, group_mid), pick(x2, group_top)]))
    x0 = times(y0 - c0, leaf, 0)
    return jnp.concatenate([rows_back(x0[None]), upper])[:, None]


def solution(mesh):
    return jax.shard_map(
        local,
        mesh=mesh,
        in_specs=(
            P(None, "cube", "front", None),
            P("cube", "front", None),
            P("cube", "front", None),
            P("cube", "front", None),
            P("cube", "front", None),
            P("cube", "front", None),
            P("cube", "front", None),
            P("cube", "front", None),
        ),
        out_specs=P(None, "cube", "front", None),
        check_vma=False,
    )
```

```python
import jax
import jax.numpy as jnp
from jax import lax
from jax.sharding import PartitionSpec as P

TILE = 64
TEAM = 4


def exchange(value, axis, mask):
    pairs = [(source, source ^ mask) for source in range(lax.axis_size(axis))]
    return lax.ppermute(value, axis, pairs)


def absolute(pieces, index, axis=0):
    if len(pieces) == 1:
        return jnp.expand_dims(pieces[0], axis)
    if len(pieces) == 2:
        return jnp.where(
            index % 2 == 0, jnp.stack(pieces, axis), jnp.stack(pieces[::-1], axis)
        )
    half = len(pieces) // 2
    first, second = (
        absolute(part, index % half, axis) for part in (pieces[:half], pieces[half:])
    )
    return jnp.where(
        index // half == 0,
        jnp.concatenate([first, second], axis),
        jnp.concatenate([second, first], axis),
    )


def team_order(pieces, g):
    join = lambda a, b: jnp.concatenate([a, b], axis=-1)
    inner = [
        jnp.where(g % 2 == 0, join(pieces[m], pieces[m + 1]), join(pieces[m + 1], pieces[m]))
        for m in (0, 2)
    ]
    return jnp.where(g // 2 == 0, join(*inner), join(inner[1], inner[0]))


def team_pieces(value, g):
    half = value.shape[-1] // 2
    sides = value[..., :half], value[..., half:]
    pieces = []
    for first, second in (sides, sides[::-1]):
        same = jnp.where(g // 2 == 0, first, second)
        parts = same[..., : half // 2], same[..., half // 2 :]
        for a, b in (parts, parts[::-1]):
            pieces.append(jnp.where(g % 2 == 0, a, b))
    return pieces


def to_parts(pieces, axis, unit):
    return [piece if m == 0 else exchange(piece, axis, m * unit) for m, piece in enumerate(pieces)]


def summed(value, axis, count, unit):
    bit = 1
    while bit < count:
        mask = 2 * bit - 1 if axis == "cube" else bit * unit
        value = value + exchange(value, axis, mask)
        bit *= 2
    return value


def times(vector, matrix, contract):
    return lax.dot_general(
        vector, matrix, (((1,), (contract,)), ((), ())), precision=lax.Precision.HIGHEST,
        preferred_element_type=jnp.float32,
    )


def local(
    right_sides,
    inverse_leaf,
    inverse_mid,
    inverse_top,
    coupling_mid,
    coupling_top,
    pattern_mid,
    pattern_top,
):
    front = lax.axis_size("front")
    cube_pos, front_pos = lax.axis_index("cube"), lax.axis_index("front")
    parts = front // TEAM
    g, q = front_pos % TEAM, front_pos // TEAM
    _, _, rows, columns = right_sides.shape
    width, half, full = columns // TEAM, TEAM * rows, front * rows
    group_mid, group_top = inverse_mid.shape[2] // full, inverse_top.shape[2] // full

    def whole_block(own, across):
        if across is None:
            across = exchange(own, "front", 2)
        beside = exchange(own, "front", 1)
        both = exchange(across, "front", 1)
        count, _, wide = own.shape
        whole = jnp.zeros((count, TEAM, rows, wide), jnp.float32)
        for m, piece in ((0, own), (1, beside), (2, across), (3, both)):
            whole = lax.dynamic_update_slice(whole, piece[:, None], (0, g ^ m, 0, 0))
        return whole.reshape(-1, wide)

    def part_pieces(inverse, count):
        return [
            jnp.concatenate([
                lax.dynamic_slice_in_dim(inverse[0], (block * parts + (q ^ m)) * half, half, 1)
                for block in range(count)
            ], axis=1)
            for m in range(parts)
        ]

    def in_order(pieces):
        return absolute(pieces, q)

    def inverse_block(inverse, count):
        pieces = to_parts(part_pieces(inverse, count), "front", TEAM)
        return whole_block(in_order(pieces), None)

    def with_cube(coupling, keep, count):
        pieces = [
            lax.dynamic_slice_in_dim(coupling[0], (cube_pos % count ^ m) * full, full, 1)
            * keep[m : m + 1]
            for m in range(count)
        ]
        pieces = to_parts(pieces, "cube", 1)
        return absolute(pieces, cube_pos % count)

    def present(tiles, start, count):
        wide = front * rows // TILE
        return [
            lax.dynamic_slice_in_dim(tiles, start + (cube_pos % count ^ m) * wide, wide, 1)
            for m in range(count)
        ]

    def own_rows(side, count):
        here = lax.broadcasted_iota(jnp.int32, (1, count, 1), 1) == cube_pos % count
        return jnp.where(here, side[:, None], 0.0).reshape(width, count * half)

    def pick(value, count):
        return lax.dynamic_slice_in_dim(value, cube_pos % count * half, half, 1)

    def rows_back(value):
        pieces = to_parts(team_pieces(value, g), "front", 1)
        turned = absolute(pieces, g, axis=1).reshape(value.shape[0], columns, rows)
        return jnp.swapaxes(turned, 1, 2)

    turned = jnp.swapaxes(right_sides[:, 0], 1, 2)
    sides = team_order(to_parts([
        lax.dynamic_slice_in_dim(turned, (g ^ m) * width, width, 1) for m in range(TEAM)
    ], "front", 1), g)

    pieces = part_pieces(inverse_leaf, 1)
    own = in_order(to_parts(pieces, "front", TEAM))
    across = in_order([exchange(piece, "front", m * TEAM + 2) for m, piece in enumerate(pieces)])
    leaf = whole_block(own, across)
    both = jnp.concatenate([pattern_mid[0], pattern_top[0]], axis=1)
    tiles = present(both, 0, group_mid) + present(both, pattern_mid.shape[2], group_top)
    wide = front * rows // TILE
    spread = lax.broadcasted_iota(jnp.int32, (wide, full), 1) // TILE
    spread = spread == lax.broadcasted_iota(jnp.int32, (wide, full), 0)
    keep = times(jnp.concatenate(tiles).astype(jnp.float32), spread.astype(jnp.float32), 0)
    couple_mid = with_cube(coupling_mid, keep[:group_mid], group_mid)
    couple_mid = whole_block(couple_mid, None)
    mid = inverse_block(inverse_mid, group_mid)
    couple_top = with_cube(coupling_top, keep[group_mid:], group_top)
    couple_top = whole_block(couple_top, None)
    top = inverse_block(inverse_top, group_top)

    y0 = summed(times(sides[0], leaf, 1), "front", parts, TEAM)
    w1 = own_rows(sides[1], group_mid) - times(y0, couple_mid, 1)
    w1 = summed(w1, "cube", group_mid, 1)
    y1 = summed(times(w1, mid, 1), "front", parts, TEAM)
    w2 = own_rows(sides[2], group_top) - times(y1, couple_top, 1)
    w2 = summed(w2, "cube", group_top, 1)
    y2 = summed(times(w2, top, 1), "front", parts, TEAM)
    x2 = summed(times(y2, top, 0), "cube", group_top, 1)
    c1 = summed(times(x2, couple_top, 0), "front", parts, TEAM)
    x1 = summed(times(y1 - c1, mid, 0), "cube", group_mid, 1)
    c0 = summed(times(x1, couple_mid, 0), "front", parts, TEAM)
    upper = rows_back(jnp.stack([pick(x1, group_mid), pick(x2, group_top)]))
    x0 = times(y0 - c0, leaf, 0)
    return jnp.concatenate([rows_back(x0[None]), upper])[:, None]


def solution(mesh):
    return jax.shard_map(
        local,
        mesh=mesh,
        in_specs=(
            P(None, "cube", "front", None),
            P("cube", "front", None),
            P("cube", "front", None),
            P("cube", "front", None),
            P("cube", "front", None),
            P("cube", "front", None),
            P("cube", "front", None),
            P("cube", "front", None),
        ),
        out_specs=P(None, "cube", "front", None),
        check_vma=False,
    )
```
